32 devices in a mesh: grp: 2 (over x), chan: 16 (over z, y, core).
Axes of the slice: x: 2, y: 2, z: 4, core: 2. Of those that a mesh axis runs over, the one named last changes fastest.
Arguments:
- traces: bfloat16 [32, 16, 256, 512], P(('grp', 'chan')), parts along dimension 0, may hold values from -6 to 6
- mask: int32 [32, 16], P('grp'), parts along dimension 0, may hold values 0 or 1
- counts: int32 [32], P('grp'), parts along dimension 0, may hold values from 0 to 5, as said below
Outputs:
- forward: float32 [32, 5, 128, 512], P(('grp', 'chan')), parts along dimension 0
- backward: float32 [32, 5, 128, 512], P(('grp', 'chan')), parts along dimension 0
The draws below stay inside these ranges and needn't reach their ends.
There are 2 independent parts, one for each index of `grp`. The reference program is written for one: setup_inputs(seed, part) draws one part's arguments, and reference() takes and returns one part's arrays. A program takes and returns all parts, laid end to end along the dimension named above; each array names one. Nothing has to cross between parts.
Inputs may be any that keep to these rules, and one draw needn't show every extreme that they name: counts[b] <= min(5, 15 - b); block 0 always has 5 partners.
All inputs are finite; a program needn't handle non-finite values.
Results may differ from the reference program's by a relative error of at most 0.0063.
Values may be sent and summed in bfloat16 or wider, within the bound.
A program may use at most 128 MiB of HBM per device.

```python
import math
import jax
import jax.numpy as jnp
from jax import lax

CH = 512
L = 256
W = 16
MAXP = 5
BLOCKS = 16


def draw_counts(key, part):
    blocks = jnp.arange(BLOCKS, dtype=jnp.int32)
    drawn = jax.random.randint(key, (BLOCKS,), 1, MAXP + 1).astype(jnp.int32)
    drawn = jnp.where(blocks == 0, MAXP, drawn)
    return jnp.minimum(drawn, BLOCKS - 1 - blocks).astype(jnp.int32)


def with_ends(entries, stream_key, smallest, high):
    spot = [jax.random.randint(jax.random.fold_in(stream_key, axis), (), 0, length) for axis, length in enumerate(entries.shape)]
    widest = entries.shape.index(max(entries.shape))
    neighbour = spot[:widest] + [(spot[widest] + 1) % entries.shape[widest]] + spot[widest + 1:]
    return entries.at[tuple(spot)].set(smallest).at[tuple(neighbour)].set(high)


def levels(key, extent, shards, low, top_value):
    def one(axis_at, blocks):
        heights = jax.random.uniform(jax.random.fold_in(jax.random.fold_in(key, 6), axis_at), (blocks,), jnp.float32, low / len(shards), top_value / len(shards))
        return jnp.repeat(jnp.exp(heights), extent[axis_at] // blocks).reshape((-1,) + (1,) * (len(extent) - axis_at - 1))

    loudness = one(*shards[0])
    for cut in shards[1:]:
        loudness = loudness * one(*cut)
    return loudness


def noise(key, dims, scale, limit, split=(), kind=jnp.bfloat16):
    factor_of = levels(key, dims, split, -0.22, 0.18) if split else 1.0
    values = jax.random.normal(key, dims, jnp.float32) * scale * factor_of
    return jnp.minimum(jnp.maximum(values, -limit), limit).astype(kind)


def setup_inputs(seed: int = 0, part: int = 0) -> dict:
    keys = jax.random.split(jax.random.key(seed), 4)
    part_keys = jax.random.split(jax.random.fold_in(keys[3], part), 4)
    traces = noise(part_keys[0], (BLOCKS, W, L, CH), 1.0, 6.0, ((0, 16),))
    mask = with_ends((jax.random.randint(part_keys[1], (BLOCKS, W), 0, 4) < 3).astype(jnp.int32), jax.random.fold_in(part_keys[1], 1), 0, 1)
    counts = draw_counts(jax.random.fold_in(jax.random.fold_in(keys[3], part), 71), part)
    return dict(traces=traces, mask=mask, counts=counts)


def lag_table(lags, bins):
    times = jnp.arange(lags, dtype=jnp.int32)[:, None]
    freqs = jnp.arange(1, bins + 1, dtype=jnp.int32)[None, :]
    phase = (times * freqs % lags).astype(jnp.float32) * (2.0 * math.pi / lags)
    return jnp.concatenate([jnp.cos(phase), -jnp.sin(phase)], axis=1).astype(jnp.bfloat16)

def whiten(record, table):
    bins = table.shape[1] // 2
    raw = jnp.einsum('tk,wtc->wkc', table.astype(jnp.float32), record.astype(jnp.float32), precision=lax.Precision.HIGHEST)
    power = lax.optimization_barrier(jnp.sum(raw * raw, axis=1)) / bins
    return (raw / jnp.sqrt(power + 1e-06)[:, None, :]).astype(jnp.bfloat16)

def stack_pair(first, second, weight):
    half = first.shape[1] // 2
    wlen = first.shape[0]
    first_re = first[:, :half].astype(jnp.float32)
    first_im = first[:, half:].astype(jnp.float32)
    second_re = second[:, :half].astype(jnp.float32)
    second_im = second[:, half:].astype(jnp.float32)
    scaled = weight[:, None, None]
    real_part = lax.optimization_barrier(jnp.sum(scaled * (first_re * second_re + first_im * second_im), axis=0))
    imag_part = lax.optimization_barrier(jnp.sum(scaled * (first_im * second_re - first_re * second_im), axis=0))
    return (jnp.concatenate([real_part, imag_part], axis=0) / math.sqrt(wlen)).astype(jnp.bfloat16)

def pair_lags(first, second, weight, table, bins):
    stacked = stack_pair(first, second, weight)
    return jnp.dot(table, stacked, preferred_element_type=jnp.float32) / math.sqrt(bins)

def reference(traces, mask, counts):
    blocks = traces.shape[0]
    lags = traces.shape[2]
    bins = lags // 2
    table = lag_table(lags, bins)
    white = lax.map(lambda record: whiten(record, table), traces)
    valid = mask.astype(jnp.float32)

    def one_block(block):
        causal = []
        acausal = []
        for step in range(1, MAXP + 1):
            other = jnp.minimum(block + step, blocks - 1).astype(jnp.int32)
            weight = valid[block] * valid[other]
            corr = pair_lags(white[block], white[other], weight, table, bins)
            corr = jnp.where(counts[block] >= step, corr, jnp.zeros_like(corr))
            causal.append(corr[:bins])
            acausal.append(corr[bins:][::-1])
        return (jnp.stack(causal), jnp.stack(acausal))
    forward, acausal_all = lax.map(one_block, jnp.arange(blocks, dtype=jnp.int32))
    rows = jnp.arange(blocks, dtype=jnp.int32)
    backward_list = []
    for step in range(1, MAXP + 1):
        rolled = jnp.roll(acausal_all[:, step - 1], step, axis=0)
        backward_list.append(jnp.where((rows >= step)[:, None, None], rolled, jnp.zeros_like(rolled)))
    backward = jnp.stack(backward_list, axis=1)
    return (forward, backward)
```

```python
import functools
import math

import numpy as np

import jax
import jax.numpy as jnp
from jax import lax
from jax.experimental import pallas as pl
from jax.experimental.pallas import tpu as pltpu
from jax.sharding import PartitionSpec as P

MAXP = 5
TEAM = 4
LANES = 128
GROUPS = 4
SLOTS = 9
TILE = 32

OWN_PAIRS = [(2, 3, 3), (3, 4, 2), (4, 5, 1)]
A_PAIRS = [(0, 2, 4), (1, 2, 4)]
B_PAIRS = [(2, 6, 2), (3, 6, 3)]
AB_PAIRS = [(1, 6, 1)]
FIRST = {}
for _runs in (OWN_PAIRS, A_PAIRS, B_PAIRS, AB_PAIRS):
    for _run in _runs:
        FIRST[_run] = sum(r[2] for r in FIRST)
PAIRS = sum(r[2] for r in FIRST)


def lag_table(lags, bins):
    times = np.arange(lags, dtype=np.int32)[:, None]
    freqs = np.arange(1, bins + 1, dtype=np.int32)[None, :]
    phase = (times * freqs % lags).astype(np.float32) * np.float32(2.0 * math.pi / lags)
    return np.concatenate([np.cos(phase), -np.sin(phase)], axis=1)


def kernel(axis, n, traces, mask, counts, table_t, table_lag, fwd_out, bwd_out,
           record, white, acc, res, back,
           t_send, t_recv, z_send, z_recv, r_send, r_recv):
    me = lax.axis_index(axis)
    team = me // TEAM
    q = me % TEAM
    base = team * TEAM
    odd = q % 2
    teams = n // TEAM
    wins = record.shape[1]
    lags = record.shape[2]
    bins = lags // 2
    chunk = wins // GROUPS
    below = team > 0
    above = team < teams - 1
    step = TEAM * (1 - 2 * odd)
    has_a = jnp.where(odd == 0, team, teams - 1 - team) > 0
    has_b = jnp.where(odd == 0, teams - 1 - team, team) > 0
    sign = (1 - 2 * odd).astype(jnp.float32)

    def block_of(slot):
        return base + jnp.where(odd == 0, slot - 2, 5 - slot)

    barrier = pltpu.get_barrier_semaphore()
    for shift in (-1, 0, 1):
        for i in range(TEAM):
            other = base + shift * TEAM + i
            there = (other >= 0) & (other < n) & (other != me)

            @pl.when(there)
            def _():
                pl.semaphore_signal(barrier, inc=1, device_id={axis: other})
    pl.semaphore_wait(barrier, TEAM - 1 + TEAM * below.astype(jnp.int32) + TEAM * above.astype(jnp.int32))

    def windows(g):
        return pl.ds(g * chunk, chunk)

    def lanes(i):
        return pl.ds(pl.multiple_of(i * LANES, LANES), LANES)

    def trace_copy(peer, g):
        return pltpu.make_async_remote_copy(
            src_ref=traces.at[0, windows(g), :, lanes(peer)],
            dst_ref=record.at[q, windows(g)],
            send_sem=t_send.at[peer, g],
            recv_sem=t_recv.at[q, g],
            device_id={axis: base + peer},
        )

    def own_copy(g):
        return pltpu.make_async_copy(traces.at[0, windows(g), :, lanes(q)], record.at[q, windows(g)], t_recv.at[q, g])

    peers = ((q + 2) % TEAM, 3 - q, q + 1 - 2 * odd)
    for g in range(GROUPS):
        own_copy(g).start()
        for peer in peers:
            trace_copy(peer, g).start()

    def to_a(u, g):
        return pltpu.make_async_remote_copy(
            src_ref=white.at[u + 2, windows(g)],
            dst_ref=white.at[u + 6, windows(g)],
            send_sem=z_send.at[u, g],
            recv_sem=z_recv.at[u + 2, g],
            device_id={axis: me - step},
        )

    def to_b(u, g):
        return pltpu.make_async_remote_copy(
            src_ref=white.at[u + 2, windows(g)],
            dst_ref=white.at[u - 2, windows(g)],
            send_sem=z_send.at[u + 1, g],
            recv_sem=z_recv.at[u - 2, g],
            device_id={axis: me + step},
        )

    def whiten_group(g):
        def one(u, carry):
            i = jnp.where(odd == 0, u, 3 - u)
            pltpu.make_async_copy(record.at[i, windows(g)], record.at[i, windows(g)], t_recv.at[i, g]).wait()
            for h in range(0, chunk, 2):
                w = g * chunk + h
                rec = jnp.concatenate([record[i, w], record[i, w + 1]], axis=1)
                raw = jnp.dot(table_t[...], rec, preferred_element_type=jnp.float32)
                power = jnp.sum(raw * raw, axis=0, keepdims=True) / bins
                inv = 1.0 / jnp.sqrt(power + 1e-06)
                for e in range(2):
                    part = slice(e * LANES, (e + 1) * LANES)
                    keep = mask[base + i, w + e].astype(jnp.float32)
                    white[u + 2, w + e] = (raw[:, part] * (inv[:, part] * keep)).astype(jnp.bfloat16)

            @pl.when((u <= 2) & has_a)
            def _():
                to_a(u, g).start()

            @pl.when((u >= 2) & has_b)
            def _():
                to_b(u, g).start()

            return carry

        lax.fori_loop(0, TEAM, one, 0)

    def stack_run(run, g):
        s, t0, count = run
        first = FIRST[run]

        def one(v, carry):
            t = t0 + v

            def tile(k, inner):
                re_at = pl.ds(pl.multiple_of(k * TILE, TILE), TILE)
                im_at = pl.ds(pl.multiple_of(bins + k * TILE, TILE), TILE)
                fresh = g == 0
                real = jnp.where(fresh, 0.0, acc[first + v, re_at, :])
                imag = jnp.where(fresh, 0.0, acc[first + v, im_at, :])
                for h in range(chunk):
                    w = g * chunk + h
                    a_re = white[s, w, re_at, :].astype(jnp.float32)
                    a_im = white[s, w, im_at, :].astype(jnp.float32)
                    b_re = white[t, w, re_at, :].astype(jnp.float32)
                    b_im = white[t, w, im_at, :].astype(jnp.float32)
                    real = real + (a_re * b_re + a_im * b_im)
                    imag = imag + (a_im * b_re - a_re * b_im)
                acc[first + v, re_at, :] = real
                acc[first + v, im_at, :] = imag
                return inner

            lax.fori_loop(0, bins // TILE, tile, 0)
            return carry

        lax.fori_loop(0, count, one, 0)

    def result_copies(s, t, index):
        early = block_of(jnp.where(odd == 0, s, t))
        late = block_of(jnp.where(odd == 0, t, s))
        out = []
        for side, owner in ((0, early), (1, late)):
            src = res.at[index, pl.ds(side * bins, bins)]
            dst = back.at[side, t - s - 1, :, lanes(q)]
            local = pltpu.make_async_copy(src, dst, r_recv.at[side, t - s - 1])
            remote = pltpu.make_async_remote_copy(
                src_ref=src, dst_ref=dst, send_sem=r_send.at[index, side],
                recv_sem=r_recv.at[side, t - s - 1], device_id={axis: owner},
            )
            out.append((owner, local, remote))
        return out

    def finish_run(run):
        s, t0, count = run
        first = FIRST[run]

        def one(v, carry):
            total = acc[first + v] * (1.0 / math.sqrt(wins))
            stacked = jnp.concatenate([total[:bins], total[bins:] * sign], axis=0).astype(jnp.bfloat16)
            corr = jnp.dot(table_lag[...], stacked, preferred_element_type=jnp.float32) * (1.0 / math.sqrt(bins))
            res[first + v] = corr.astype(jnp.bfloat16)
            for owner, local, remote in result_copies(s, t0 + v, first + v):
                @pl.when(owner == me)
                def _():
                    local.start()

                @pl.when(owner != me)
                def _():
                    remote.start()
            return carry

        lax.fori_loop(0, count, one, 0)

    def finish_sends(run):
        s, t0, count = run
        first = FIRST[run]

        def one(v, carry):
            for owner, local, remote in result_copies(s, t0 + v, first + v):
                @pl.when(owner != me)
                def _():
                    remote.wait_send()
            return carry

        lax.fori_loop(0, count, one, 0)

    def arrived(z, slot, g):
        view = white.at[slot, windows(g)]
        pltpu.make_async_copy(view, view, z_recv.at[z, g]).wait()

    def phase(g, carry):
        @pl.when(g < GROUPS)
        def _():
            whiten_group(g)
            for run in OWN_PAIRS:
                stack_run(run, g)

        @pl.when(g == GROUPS)
        def _():
            for run in OWN_PAIRS:
                finish_run(run)

        @pl.when(g >= 1)
        def _():
            @pl.when(has_a)
            def _():
                for z in range(2):
                    arrived(z, z, g - 1)
                for run in A_PAIRS:
                    stack_run(run, g - 1)

            @pl.when(has_b)
            def _():
                for z in range(2, 5):
                    arrived(z, z + 4, g - 1)
                for run in B_PAIRS:
                    stack_run(run, g - 1)

            @pl.when(has_a & has_b)
            def _():
                for run in AB_PAIRS:
                    stack_run(run, g - 1)

        return carry

    lax.fori_loop(0, GROUPS + 1, phase, 0)

    @pl.when(has_a)
    def _():
        for run in A_PAIRS:
            finish_run(run)

    @pl.when(has_b)
    def _():
        for run in B_PAIRS:
            finish_run(run)

    @pl.when(has_a & has_b)
    def _():
        for run in AB_PAIRS:
            finish_run(run)

    def sent(g, carry):
        for peer in peers:
            trace_copy(peer, g).wait_send()

        @pl.when(has_a)
        def _():
            for u in range(3):
                to_a(u, g).wait_send()

        @pl.when(has_b)
        def _():
            for u in range(2, 4):
                to_b(u, g).wait_send()

        return carry

    lax.fori_loop(0, GROUPS, sent, 0)
    for j in range(MAXP):
        for side, there in ((0, me + j + 1 < n), (1, me - j - 1 >= 0)):
            @pl.when(there)
            def _():
                view = back.at[side, j]
                pltpu.make_async_copy(view, view, r_recv.at[side, j]).wait()
        reach = counts[me] >= j + 1
        fwd_out[0, j] = jnp.where(reach, back[0, j], jnp.bfloat16(0))
        source = jnp.maximum(me - j - 1, 0)
        reached = (counts[source] >= j + 1) & (me >= j + 1)
        bwd_out[0, j] = jnp.where(reached, back[1, j], jnp.bfloat16(0))
    for run in OWN_PAIRS:
        finish_sends(run)

    @pl.when(has_a)
    def _():
        for run in A_PAIRS:
            finish_sends(run)

    @pl.when(has_b)
    def _():
        for run in B_PAIRS:
            finish_sends(run)

    @pl.when(has_a & has_b)
    def _():
        for run in AB_PAIRS:
            finish_sends(run)


def local(traces, mask, counts):
    axis = "chan"
    n = lax.axis_size(axis)
    _, wins, lags, width = traces.shape
    bins = lags // 2
    table = lag_table(lags, bins)
    table_lag = np.concatenate([table[:bins], table[bins:][::-1]], axis=0)
    half = jax.ShapeDtypeStruct((1, MAXP, bins, width), jnp.bfloat16)
    vmem = pl.BlockSpec(memory_space=pltpu.VMEM)
    smem = pl.BlockSpec(memory_space=pltpu.SMEM)
    forward, backward = pl.pallas_call(
        functools.partial(kernel, axis, n),
        out_shape=(half, half),
        in_specs=[pl.BlockSpec(memory_space=pl.ANY), smem, smem, vmem, vmem],
        out_specs=(vmem, vmem),
        scratch_shapes=[
            pltpu.VMEM((TEAM, wins, lags, LANES), jnp.bfloat16),
            pltpu.VMEM((SLOTS, wins, lags, LANES), jnp.bfloat16),
            pltpu.VMEM((PAIRS, lags, LANES), jnp.float32),
            pltpu.VMEM((PAIRS, lags, LANES), jnp.bfloat16),
            pltpu.VMEM((2, MAXP, bins, width), jnp.bfloat16),
            pltpu.SemaphoreType.DMA((TEAM, GROUPS)),
            pltpu.SemaphoreType.DMA((TEAM, GROUPS)),
            pltpu.SemaphoreType.DMA((5, GROUPS)),
            pltpu.SemaphoreType.DMA((5, GROUPS)),
            pltpu.SemaphoreType.DMA((PAIRS, 2)),
            pltpu.SemaphoreType.DMA((2, MAXP)),
        ],
        compiler_params=pltpu.CompilerParams(collective_id=0, has_side_effects=True, vmem_limit_bytes=48 << 20),
        name="xcorr",
    )(traces, mask, counts, jnp.asarray(table.T, jnp.bfloat16), jnp.asarray(table_lag, jnp.bfloat16))
    return forward.astype(jnp.float32), backward.astype(jnp.float32)


def solution(mesh):
    return jax.shard_map(
        local,
        mesh=mesh,
        in_specs=(P(("grp", "chan"), None, None, None), P("grp", None), P("grp")),
        out_specs=(P(("grp", "chan"), None, None, None), P(("grp", "chan"), None, None, None)),
        check_vma=False,
    )
```

```python
import functools
import math

import numpy as np

import jax
import jax.numpy as jnp
from jax import lax
from jax.experimental import pallas as pl
from jax.experimental.pallas import tpu as pltpu
from jax.sharding import PartitionSpec as P

MAXP = 5
TEAM = 4
LANES = 128
GROUPS = 4
SLOTS = 9
TILE = 32

OWN_PAIRS = [(2, 3, 3), (3, 4, 2), (4, 5, 1)]
A_PAIRS = [(0, 2, 4), (1, 2, 4)]
B_PAIRS = [(2, 6, 2), (3, 6, 2)]
C_PAIRS = [(3, 8, 1)]
AB_PAIRS = [(1, 6, 1)]
FIRST = {}
for _runs in (OWN_PAIRS, A_PAIRS, B_PAIRS, C_PAIRS, AB_PAIRS):
    for _run in _runs:
        FIRST[_run] = sum(r[2] for r in FIRST)
PAIRS = sum(r[2] for r in FIRST)


def lag_table(lags, bins):
    times = np.arange(lags, dtype=np.int32)[:, None]
    freqs = np.arange(1, bins + 1, dtype=np.int32)[None, :]
    phase = (times * freqs % lags).astype(np.float32) * np.float32(2.0 * math.pi / lags)
    return np.concatenate([np.cos(phase), -np.sin(phase)], axis=1)


def kernel(axis, n, traces, mask_in, counts_in, table_t_in, table_lag_in, fwd_out, bwd_out,
           mask, counts, table_t, table_lag, fetch, record, white, acc, res, back,
           t_send, t_recv, z_send, z_recv, r_send, r_recv):
    me = lax.axis_index(axis)
    team = me // TEAM
    q = me % TEAM
    base = team * TEAM
    odd = q % 2
    teams = n // TEAM
    wins = record.shape[1]
    lags = record.shape[2]
    bins = lags // 2
    chunk = wins // GROUPS
    below = team > 0
    above = team < teams - 1
    step = TEAM * (1 - 2 * odd)
    has_a = jnp.where(odd == 0, team, teams - 1 - team) > 0
    has_b = jnp.where(odd == 0, teams - 1 - team, team) > 0
    sign = (1 - 2 * odd).astype(jnp.float32)

    def block_of(slot):
        return base + jnp.where(odd == 0, slot - 2, 5 - slot)

    fetches = [
        pltpu.make_async_copy(src, dst, fetch.at[k])
        for k, (src, dst) in enumerate(
            ((table_t_in, table_t), (mask_in, mask), (table_lag_in, table_lag), (counts_in, counts)))
    ]
    for copy in fetches:
        copy.start()
    early_low = (q % 3) == 0
    first = jnp.where(early_low, 0, 2)
    barrier = pltpu.get_barrier_semaphore()
    for shift in (-1, 0, 1):
        for i in range(TEAM):
            other = base + shift * TEAM + i
            there = (other >= 0) & (other < n) & (other != me)

            @pl.when(there)
            def _():
                pl.semaphore_signal(barrier, inc=1, device_id={axis: other})
    pl.semaphore_wait(barrier, TEAM - 1 + TEAM * below.astype(jnp.int32) + TEAM * above.astype(jnp.int32))

    def windows(g):
        return pl.ds(g * chunk, chunk)

    def lanes(i):
        return pl.ds(pl.multiple_of(i * LANES, LANES), LANES)

    def trace_copy(peer, g):
        return pltpu.make_async_remote_copy(
            src_ref=traces.at[0, windows(g), :, lanes(peer)],
            dst_ref=record.at[q, windows(g)],
            send_sem=t_send.at[peer, g],
            recv_sem=t_recv.at[q, g],
            device_id={axis: base + peer},
        )

    def own_copy(g):
        return pltpu.make_async_copy(traces.at[0, windows(g), :, lanes(q)], record.at[q, windows(g)], t_recv.at[q, g])

    peers = ((q + 2) % TEAM, 3 - q, q + 1 - 2 * odd)
    for g in range(GROUPS):
        own_copy(g).start()
        for peer in peers:
            trace_copy(peer, g).start()

    def to_a(u, g):
        return pltpu.make_async_remote_copy(
            src_ref=white.at[u + 2, windows(g)],
            dst_ref=white.at[u + 6, windows(g)],
            send_sem=z_send.at[u, g],
            recv_sem=z_recv.at[u + 2, g],
            device_id={axis: me - step},
        )

    def to_b(u, g):
        return pltpu.make_async_remote_copy(
            src_ref=white.at[u + 2, windows(g)],
            dst_ref=white.at[u - 2, windows(g)],
            send_sem=z_send.at[u + 1, g],
            recv_sem=z_recv.at[u - 2, g],
            device_id={axis: me + step},
        )

    def whiten_group(u0, g):
        def one(v, carry):
            u = u0 + v
            i = jnp.where(odd == 0, u, 3 - u)
            pltpu.make_async_copy(record.at[i, windows(g)], record.at[i, windows(g)], t_recv.at[i, g]).wait()
            for h in range(0, chunk, 2):
                w = g * chunk + h
                rec = jnp.concatenate([record[i, w], record[i, w + 1]], axis=1)
                raw = jnp.dot(table_t[...], rec, preferred_element_type=jnp.float32)
                power = jnp.sum(raw * raw, axis=0, keepdims=True) / bins
                inv = 1.0 / jnp.sqrt(power + 1e-06)
                for e in range(2):
                    part = slice(e * LANES, (e + 1) * LANES)
                    keep = mask[base + i, w + e].astype(jnp.float32)
                    white[u + 2, w + e] = (raw[:, part] * (inv[:, part] * keep)).astype(jnp.bfloat16)

            @pl.when((u <= 2) & has_a)
            def _():
                to_a(u, g).start()

            @pl.when((u >= 2) & has_b)
            def _():
                to_b(u, g).start()

            return carry

        lax.fori_loop(0, 2, one, 0)

    def stack_run(run, g):
        s, t0, count = run
        place = FIRST[run]

        def one(v, carry):
            t = t0 + v

            def tile(k, inner):
                re_at = pl.ds(pl.multiple_of(k * TILE, TILE), TILE)
                im_at = pl.ds(pl.multiple_of(bins + k * TILE, TILE), TILE)
                fresh = g == 0
                real = jnp.where(fresh, 0.0, acc[place + v, re_at, :])
                imag = jnp.where(fresh, 0.0, acc[place + v, im_at, :])
                for h in range(chunk):
                    w = g * chunk + h
                    a_re = white[s, w, re_at, :].astype(jnp.float32)
                    a_im = white[s, w, im_at, :].astype(jnp.float32)
                    b_re = white[t, w, re_at, :].astype(jnp.float32)
                    b_im = white[t, w, im_at, :].astype(jnp.float32)
                    real = real + (a_re * b_re + a_im * b_im)
                    imag = imag + (a_im * b_re - a_re * b_im)
                acc[place + v, re_at, :] = real
                acc[place + v, im_at, :] = imag
                return inner

            lax.fori_loop(0, bins // TILE, tile, 0)
            return carry

        lax.fori_loop(0, count, one, 0)

    def result_copies(s, t, index):
        early = block_of(jnp.where(odd == 0, s, t))
        late = block_of(jnp.where(odd == 0, t, s))
        out = []
        for side, owner in ((0, early), (1, late)):
            src = res.at[index, pl.ds(side * bins, bins)]
            dst = back.at[side, t - s - 1, :, lanes(q)]
            local = pltpu.make_async_copy(src, dst, r_recv.at[side, t - s - 1])
            remote = pltpu.make_async_remote_copy(
                src_ref=src, dst_ref=dst, send_sem=r_send.at[index, side],
                recv_sem=r_recv.at[side, t - s - 1], device_id={axis: owner},
            )
            out.append((owner, local, remote))
        return out

    def finish_run(run):
        s, t0, count = run
        place = FIRST[run]

        def one(v, carry):
            total = acc[place + v] * (1.0 / math.sqrt(wins))
            stacked = jnp.concatenate([total[:bins], total[bins:] * sign], axis=0).astype(jnp.bfloat16)
            corr = jnp.dot(table_lag[...], stacked, preferred_element_type=jnp.float32) * (1.0 / math.sqrt(bins))
            res[place + v] = corr.astype(jnp.bfloat16)
            for owner, local, remote in result_copies(s, t0 + v, place + v):
                @pl.when(owner == me)
                def _():
                    local.start()

                @pl.when(owner != me)
                def _():
                    remote.start()
            return carry

        lax.fori_loop(0, count, one, 0)

    def finish_sends(run):
        s, t0, count = run
        place = FIRST[run]

        def one(v, carry):
            for owner, local, remote in result_copies(s, t0 + v, place + v):
                @pl.when(owner != me)
                def _():
                    remote.wait_send()
            return carry

        lax.fori_loop(0, count, one, 0)

    def arrived(z, slot, g):
        view = white.at[slot, windows(g)]
        pltpu.make_async_copy(view, view, z_recv.at[z, g]).wait()

    def near(g, carry):
        whiten_group(first, g)
        return carry

    def far(g, carry):
        whiten_group(2 - first, g)
        for run in OWN_PAIRS:
            stack_run(run, g)
        return carry

    for copy in fetches[:2]:
        copy.wait()
    lax.fori_loop(0, GROUPS, near, 0)
    lax.fori_loop(0, GROUPS, far, 0)
    fetches[2].wait()
    for run in OWN_PAIRS:
        finish_run(run)

    def group(ready, zs, runs):
        @pl.when(ready)
        def _():
            def one(g, carry):
                for z in zs:
                    arrived(z, z if z < 2 else z + 4, g)
                for run in runs:
                    stack_run(run, g)
                return carry

            lax.fori_loop(0, GROUPS, one, 0)
            for run in runs:
                finish_run(run)

    def half(p, carry):
        low = (p == 0) == early_low
        group(low & has_b, (2, 3), B_PAIRS)
        group(jnp.logical_not(low) & has_a, (0, 1), A_PAIRS)
        group(jnp.logical_not(low) & has_b, (4,), C_PAIRS)
        return carry

    lax.fori_loop(0, 2, half, 0)
    group(has_a & has_b, (), AB_PAIRS)

    def sent(g, carry):
        for peer in peers:
            trace_copy(peer, g).wait_send()

        @pl.when(has_a)
        def _():
            for u in range(3):
                to_a(u, g).wait_send()

        @pl.when(has_b)
        def _():
            for u in range(2, 4):
                to_b(u, g).wait_send()

        return carry

    lax.fori_loop(0, GROUPS, sent, 0)
    fetches[3].wait()
    for j in range(MAXP):
        for side, there in ((0, me + j + 1 < n), (1, me - j - 1 >= 0)):
            @pl.when(there)
            def _():
                view = back.at[side, j]
                pltpu.make_async_copy(view, view, r_recv.at[side, j]).wait()
        reach = counts[me] >= j + 1
        fwd_out[0, j] = jnp.where(reach, back[0, j], jnp.bfloat16(0))
        source = jnp.maximum(me - j - 1, 0)
        reached = (counts[source] >= j + 1) & (me >= j + 1)
        bwd_out[0, j] = jnp.where(reached, back[1, j], jnp.bfloat16(0))
    for run in OWN_PAIRS:
        finish_sends(run)

    @pl.when(has_a)
    def _():
        for run in A_PAIRS:
            finish_sends(run)

    @pl.when(has_b)
    def _():
        for run in B_PAIRS + C_PAIRS:
            finish_sends(run)

    @pl.when(has_a & has_b)
    def _():
        for run in AB_PAIRS:
            finish_sends(run)


def local(traces, mask, counts):
    axis = "chan"
    n = lax.axis_size(axis)
    _, wins, lags, width = traces.shape
    bins = lags // 2
    table = lag_table(lags, bins)
    table_lag = np.concatenate([table[:bins], table[bins:][::-1]], axis=0)
    half = jax.ShapeDtypeStruct((1, MAXP, bins, width), jnp.bfloat16)
    vmem = pl.BlockSpec(memory_space=pltpu.VMEM)
    forward, backward = pl.pallas_call(
        functools.partial(kernel, axis, n),
        out_shape=(half, half),
        in_specs=[pl.BlockSpec(memory_space=pltpu.HBM)] * 5,
        out_specs=(vmem, vmem),
        scratch_shapes=[
            pltpu.SMEM(mask.shape, jnp.int32),
            pltpu.SMEM(counts.shape, jnp.int32),
            pltpu.VMEM((lags, lags), jnp.bfloat16),
            pltpu.VMEM((lags, lags), jnp.bfloat16),
            pltpu.SemaphoreType.DMA((4,)),
            pltpu.VMEM((TEAM, wins, lags, LANES), jnp.bfloat16),
            pltpu.VMEM((SLOTS, wins, lags, LANES), jnp.bfloat16),
            pltpu.VMEM((PAIRS, lags, LANES), jnp.float32),
            pltpu.VMEM((PAIRS, lags, LANES), jnp.bfloat16),
            pltpu.VMEM((2, MAXP, bins, width), jnp.bfloat16),
            pltpu.SemaphoreType.DMA((TEAM, GROUPS)),
            pltpu.SemaphoreType.DMA((TEAM, GROUPS)),
            pltpu.SemaphoreType.DMA((5, GROUPS)),
            pltpu.SemaphoreType.DMA((5, GROUPS)),
            pltpu.SemaphoreType.DMA((PAIRS, 2)),
            pltpu.SemaphoreType.DMA((2, MAXP)),
        ],
        compiler_params=pltpu.CompilerParams(collective_id=0, has_side_effects=True, vmem_limit_bytes=60 << 20),
        name="xcorr",
    )(traces, mask, counts, jnp.asarray(table.T, jnp.bfloat16), jnp.asarray(table_lag, jnp.bfloat16))
    return forward.astype(jnp.float32), backward.astype(jnp.float32)


def solution(mesh):
    return jax.shard_map(
        local,
        mesh=mesh,
        in_specs=(P(("grp", "chan"), None, None, None), P("grp", None), P("grp")),
        out_specs=(P(("grp", "chan"), None, None, None), P(("grp", "chan"), None, None, None)),
        check_vma=False,
    )
```

```python
import functools
import math

import numpy as np

import jax
import jax.numpy as jnp
from jax import lax
from jax.experimental import pallas as pl
from jax.experimental.pallas import tpu as pltpu
from jax.sharding import PartitionSpec as P

MAXP = 5
TEAM = 4
LANES = 128
GROUPS = 4
SLOTS = 9
TILE = 32
SPAN = 5

OWN_PAIRS = [(2, 3, 3), (3, 4, 2), (4, 5, 1)]
A_PAIRS = [(0, 2, 4), (1, 2, 4)]
B_PAIRS = [(2, 6, 2), (3, 6, 2)]
C_PAIRS = [(3, 8, 1)]
AB_PAIRS = [(1, 6, 1)]
FIRST = {}
for _runs in (OWN_PAIRS, A_PAIRS, B_PAIRS, C_PAIRS, AB_PAIRS):
    for _run in _runs:
        FIRST[_run] = sum(r[2] for r in FIRST)
PAIRS = sum(r[2] for r in FIRST)


def lag_table(lags, bins):
    times = np.arange(lags, dtype=np.int32)[:, None]
    freqs = np.arange(1, bins + 1, dtype=np.int32)[None, :]
    phase = (times * freqs % lags).astype(np.float32) * np.float32(2.0 * math.pi / lags)
    return np.concatenate([np.cos(phase), -np.sin(phase)], axis=1)


def kernel(axis, n, traces, mask_in, counts_in, table_t_in, table_lag_in, fwd_out, bwd_out,
           mask, counts, table_t, table_lag, fetch, record, white, acc, res, back,
           ready, o_sem, t_send, t_recv, z_send, z_recv, r_send, r_recv):
    me = lax.axis_index(axis)
    team = me // TEAM
    q = me % TEAM
    base = team * TEAM
    odd = q % 2
    teams = n // TEAM
    wins = record.shape[1]
    lags = record.shape[2]
    bins = lags // 2
    chunk = wins // GROUPS
    below = team > 0
    above = team < teams - 1
    step = TEAM * (1 - 2 * odd)
    has_a = jnp.where(odd == 0, team, teams - 1 - team) > 0
    has_b = jnp.where(odd == 0, teams - 1 - team, team) > 0
    sign = (1 - 2 * odd).astype(jnp.float32)

    def block_of(slot):
        return base + jnp.where(odd == 0, slot - 2, 5 - slot)

    fetches = [
        pltpu.make_async_copy(src, dst, fetch.at[k])
        for k, (src, dst) in enumerate(
            ((table_t_in, table_t), (mask_in, mask), (table_lag_in, table_lag), (counts_in, counts)))
    ]
    for copy in fetches:
        copy.start()
    early_low = (q % 3) == 0
    first = jnp.where(early_low, 0, 2)
    barrier = pltpu.get_barrier_semaphore()
    for shift in (-1, 0, 1):
        for i in range(TEAM):
            other = base + shift * TEAM + i
            there = (other >= 0) & (other < n) & (other != me)

            @pl.when(there)
            def _():
                pl.semaphore_signal(barrier, inc=1, device_id={axis: other})

    def windows(g):
        return pl.ds(g * chunk, chunk)

    def lanes(i):
        return pl.ds(pl.multiple_of(i * LANES, LANES), LANES)

    def trace_copy(peer, g):
        return pltpu.make_async_remote_copy(
            src_ref=traces.at[0, windows(g), :, lanes(peer)],
            dst_ref=record.at[q, windows(g)],
            send_sem=t_send.at[peer, g],
            recv_sem=t_recv.at[q, g],
            device_id={axis: base + peer},
        )

    def own_copy(g):
        return pltpu.make_async_copy(traces.at[0, windows(g), :, lanes(q)], record.at[q, windows(g)], t_recv.at[q, g])

    peers = ((q + 2) % TEAM, 3 - q, q + 1 - 2 * odd)
    for g in range(GROUPS):
        own_copy(g).start()

    def to_a(u, g):
        return pltpu.make_async_remote_copy(
            src_ref=white.at[u + 2, windows(g)],
            dst_ref=white.at[u + 6, windows(g)],
            send_sem=z_send.at[u, g],
            recv_sem=z_recv.at[u + 2, g],
            device_id={axis: me - step},
        )

    def to_b(u, g):
        return pltpu.make_async_remote_copy(
            src_ref=white.at[u + 2, windows(g)],
            dst_ref=white.at[u - 2, windows(g)],
            send_sem=z_send.at[u + 1, g],
            recv_sem=z_recv.at[u - 2, g],
            device_id={axis: me + step},
        )

    own_slot = jnp.where(odd == 0, q, 3 - q)

    def whiten_block(u, g):
        i = jnp.where(odd == 0, u, 3 - u)
        pltpu.make_async_copy(record.at[i, windows(g)], record.at[i, windows(g)], t_recv.at[i, g]).wait()
        for h in range(0, chunk, 2):
            w = g * chunk + h
            rec = jnp.concatenate([record[i, w], record[i, w + 1]], axis=1)
            raw = jnp.dot(table_t[...], rec, preferred_element_type=jnp.float32)
            power = jnp.sum(raw * raw, axis=0, keepdims=True) / bins
            inv = 1.0 / jnp.sqrt(power + 1e-06)
            for e in range(2):
                part = slice(e * LANES, (e + 1) * LANES)
                keep = mask[base + i, w + e].astype(jnp.float32)
                white[u + 2, w + e] = (raw[:, part] * (inv[:, part] * keep)).astype(jnp.bfloat16)

    def pass_on(u, g):
        @pl.when((u <= 2) & has_a)
        def _():
            to_a(u, g).start()

        @pl.when((u >= 2) & has_b)
        def _():
            to_b(u, g).start()

    def block_chunks(u, start):
        def one(g, carry):
            whiten_block(u, g)
            pass_on(u, g)
            return carry

        lax.fori_loop(start, GROUPS, one, 0)

    def stack_run(run, g):
        s, t0, count = run
        place = FIRST[run]

        def one(v, carry):
            t = t0 + v

            def tile(k, inner):
                re_at = pl.ds(pl.multiple_of(k * TILE, TILE), TILE)
                im_at = pl.ds(pl.multiple_of(bins + k * TILE, TILE), TILE)
                fresh = g == 0
                real = jnp.where(fresh, 0.0, acc[place + v, re_at, :])
                imag = jnp.where(fresh, 0.0, acc[place + v, im_at, :])
                for h in range(chunk):
                    w = g * chunk + h
                    a_re = white[s, w, re_at, :].astype(jnp.float32)
                    a_im = white[s, w, im_at, :].astype(jnp.float32)
                    b_re = white[t, w, re_at, :].astype(jnp.float32)
                    b_im = white[t, w, im_at, :].astype(jnp.float32)
                    real = real + (a_re * b_re + a_im * b_im)
                    imag = imag + (a_im * b_re - a_re * b_im)
                acc[place + v, re_at, :] = real
                acc[place + v, im_at, :] = imag
                return inner

            lax.fori_loop(0, bins // TILE, tile, 0)
            return carry

        lax.fori_loop(0, count, one, 0)

    def result_copies(s, t, index):
        early = block_of(jnp.where(odd == 0, s, t))
        late = block_of(jnp.where(odd == 0, t, s))
        out = []
        for side, owner in ((0, early), (1, late)):
            src = res.at[index, pl.ds(side * bins, bins)]
            dst = back.at[side, t - s - 1, :, lanes(q)]
            local = pltpu.make_async_copy(src, dst, r_recv.at[side, t - s - 1])
            remote = pltpu.make_async_remote_copy(
                src_ref=src, dst_ref=dst, send_sem=r_send.at[index, side],
                recv_sem=r_recv.at[side, t - s - 1], device_id={axis: owner},
            )
            out.append((owner, local, remote))
        return out

    def finish_run(run):
        s, t0, count = run
        place = FIRST[run]

        def one(v, carry):
            total = acc[place + v] * (1.0 / math.sqrt(wins))
            stacked = jnp.concatenate([total[:bins], total[bins:] * sign], axis=0).astype(jnp.bfloat16)
            corr = jnp.dot(table_lag[...], stacked, preferred_element_type=jnp.float32) * (1.0 / math.sqrt(bins))
            res[place + v] = corr.astype(jnp.bfloat16)
            for owner, local, remote in result_copies(s, t0 + v, place + v):
                @pl.when(owner == me)
                def _():
                    local.start()

                @pl.when(owner != me)
                def _():
                    remote.start()
            return carry

        lax.fori_loop(0, count, one, 0)

    def finish_sends(run):
        s, t0, count = run
        place = FIRST[run]

        def one(v, carry):
            for owner, local, remote in result_copies(s, t0 + v, place + v):
                @pl.when(owner != me)
                def _():
                    remote.wait_send()
            return carry

        lax.fori_loop(0, count, one, 0)

    def arrived(z, slot, g):
        view = white.at[slot, windows(g)]
        pltpu.make_async_copy(view, view, z_recv.at[z, g]).wait()

    def far(g, carry):
        for v in range(2):
            whiten_block(2 - first + v, g)
            pass_on(2 - first + v, g)
        for run in OWN_PAIRS:
            stack_run(run, g)
        return carry

    for copy in fetches[:2]:
        copy.wait()
    whiten_block(own_slot, 0)
    pl.semaphore_wait(barrier, TEAM - 1 + TEAM * below.astype(jnp.int32) + TEAM * above.astype(jnp.int32))
    pass_on(own_slot, 0)
    for g in range(GROUPS):
        for peer in peers:
            trace_copy(peer, g).start()
    block_chunks(own_slot, 1)
    block_chunks(2 * first + 1 - own_slot, 0)
    lax.fori_loop(0, GROUPS, far, 0)
    fetches[2].wait()
    for run in OWN_PAIRS:
        finish_run(run)

    def group(ready, zs, runs):
        @pl.when(ready)
        def _():
            def one(g, carry):
                for z in zs:
                    arrived(z, z if z < 2 else z + 4, g)
                for run in runs:
                    stack_run(run, g)
                return carry

            lax.fori_loop(0, GROUPS, one, 0)
            for run in runs:
                finish_run(run)

    def half(p, carry):
        low = (p == 0) == early_low
        group(low & has_b, (2, 3), B_PAIRS)
        group(jnp.logical_not(low) & has_a, (0, 1), A_PAIRS)
        group(jnp.logical_not(low) & has_b, (4,), C_PAIRS)
        return carry

    lax.fori_loop(0, 2, half, 0)
    group(has_a & has_b, (), AB_PAIRS)

    def sent(g, carry):
        for peer in peers:
            trace_copy(peer, g).wait_send()

        @pl.when(has_a)
        def _():
            for u in range(3):
                to_a(u, g).wait_send()

        @pl.when(has_b)
        def _():
            for u in range(2, 4):
                to_b(u, g).wait_send()

        return carry

    lax.fori_loop(0, GROUPS, sent, 0)
    fetches[3].wait()
    for j in range(MAXP):
        for side, there in ((0, me + j + 1 < n), (1, me - j - 1 >= 0)):
            @pl.when(there)
            def _():
                view = back.at[side, j]
                pltpu.make_async_copy(view, view, r_recv.at[side, j]).wait()
        reach = counts[me] >= j + 1
        ready[0, j] = jnp.where(reach, back[0, j], jnp.bfloat16(0))
        pltpu.make_async_copy(ready.at[0, j], fwd_out.at[0, j], o_sem.at[0, j]).start()
        source = jnp.maximum(me - j - 1, 0)
        reached = (counts[source] >= j + 1) & (me >= j + 1)
        ready[1, j] = jnp.where(reached, back[1, j], jnp.bfloat16(0))
        pltpu.make_async_copy(ready.at[1, j], bwd_out.at[0, j], o_sem.at[1, j]).start()
    for run in OWN_PAIRS:
        finish_sends(run)

    @pl.when(has_a)
    def _():
        for run in A_PAIRS:
            finish_sends(run)

    @pl.when(has_b)
    def _():
        for run in B_PAIRS + C_PAIRS:
            finish_sends(run)

    @pl.when(has_a & has_b)
    def _():
        for run in AB_PAIRS:
            finish_sends(run)
    for j in range(MAXP):
        pltpu.make_async_copy(ready.at[0, j], fwd_out.at[0, j], o_sem.at[0, j]).wait()
        pltpu.make_async_copy(ready.at[1, j], bwd_out.at[0, j], o_sem.at[1, j]).wait()


def widen(fwd, bwd, fwd_out, bwd_out):
    fwd_out[...] = fwd[...].astype(jnp.float32)
    bwd_out[...] = bwd[...].astype(jnp.float32)


def local(traces, mask, counts):
    axis = "chan"
    n = lax.axis_size(axis)
    _, wins, lags, width = traces.shape
    bins = lags // 2
    table = lag_table(lags, bins)
    table_lag = np.concatenate([table[:bins], table[bins:][::-1]], axis=0)
    half = jax.ShapeDtypeStruct((1, MAXP, bins, width), jnp.bfloat16)
    forward, backward = pl.pallas_call(
        functools.partial(kernel, axis, n),
        out_shape=(half, half),
        in_specs=[pl.BlockSpec(memory_space=pltpu.HBM)] * 5,
        out_specs=[pl.BlockSpec(memory_space=pltpu.HBM)] * 2,
        scratch_shapes=[
            pltpu.SMEM(mask.shape, jnp.int32),
            pltpu.SMEM(counts.shape, jnp.int32),
            pltpu.VMEM((lags, lags), jnp.bfloat16),
            pltpu.VMEM((lags, lags), jnp.bfloat16),
            pltpu.SemaphoreType.DMA((4,)),
            pltpu.VMEM((TEAM, wins, lags, LANES), jnp.bfloat16),
            pltpu.VMEM((SLOTS, wins, lags, LANES), jnp.bfloat16),
            pltpu.VMEM((PAIRS, lags, LANES), jnp.float32),
            pltpu.VMEM((PAIRS, lags, LANES), jnp.bfloat16),
            pltpu.VMEM((2, MAXP, bins, width), jnp.bfloat16),
            pltpu.VMEM((2, MAXP, bins, width), jnp.bfloat16),
            pltpu.SemaphoreType.DMA((2, MAXP)),
            pltpu.SemaphoreType.DMA((TEAM, GROUPS)),
            pltpu.SemaphoreType.DMA((TEAM, GROUPS)),
            pltpu.SemaphoreType.DMA((5, GROUPS)),
            pltpu.SemaphoreType.DMA((5, GROUPS)),
            pltpu.SemaphoreType.DMA((PAIRS, 2)),
            pltpu.SemaphoreType.DMA((2, MAXP)),
        ],
        compiler_params=pltpu.CompilerParams(collective_id=0, has_side_effects=True, vmem_limit_bytes=60 << 20),
        name="xcorr",
    )(traces, mask, counts, jnp.asarray(table.T, jnp.bfloat16), jnp.asarray(table_lag, jnp.bfloat16))
    lag_block = pl.BlockSpec((1, SPAN, bins, width), lambda j: (0, j, 0, 0))
    wide = jax.ShapeDtypeStruct(half.shape, jnp.float32)
    return pl.pallas_call(
        widen,
        grid=(MAXP // SPAN,),
        out_shape=(wide, wide),
        in_specs=[lag_block, lag_block],
        out_specs=(lag_block, lag_block),
        name="widen",
    )(forward, backward)


def solution(mesh):
    return jax.shard_map(
        local,
        mesh=mesh,
        in_specs=(P(("grp", "chan"), None, None, None), P("grp", None), P("grp")),
        out_specs=(P(("grp", "chan"), None, None, None), P(("grp", "chan"), None, None, None)),
        check_vma=False,
    )
```

```python
import functools
import math

import numpy as np

import jax
import jax.numpy as jnp
from jax import lax
from jax.experimental import pallas as pl
from jax.experimental.pallas import tpu as pltpu
from jax.sharding import PartitionSpec as P

MAXP = 5
TEAM = 4
LANES = 128
GROUPS = 4
SLOTS = 9
TILE = 32
SPAN = 5

OWN_PAIRS = [(2, 3, 3), (3, 4, 2), (4, 5, 1)]
A_PAIRS = [(0, 2, 4), (1, 2, 4)]
B_PAIRS = [(2, 6, 2), (3, 6, 2)]
C_PAIRS = [(3, 8, 1)]
AB_PAIRS = [(1, 6, 1)]
FIRST = {}
for _runs in (OWN_PAIRS, A_PAIRS, B_PAIRS, C_PAIRS, AB_PAIRS):
    for _run in _runs:
        FIRST[_run] = sum(r[2] for r in FIRST)
PAIRS = sum(r[2] for r in FIRST)


def lag_table(lags, bins):
    times = np.arange(lags, dtype=np.int32)[:, None]
    freqs = np.arange(1, bins + 1, dtype=np.int32)[None, :]
    phase = (times * freqs % lags).astype(np.float32) * np.float32(2.0 * math.pi / lags)
    return np.concatenate([np.cos(phase), -np.sin(phase)], axis=1)


def kernel(axis, n, traces, mask_in, counts_in, table_t_in, table_lag_in, fwd_out, bwd_out,
           mask, counts, table_t, table_lag, fetch, record, white, acc, res, back,
           ready, o_sem, t_send, t_recv, z_send, z_recv, r_send, r_recv):
    me = lax.axis_index(axis)
    team = me // TEAM
    q = me % TEAM
    base = team * TEAM
    odd = q % 2
    teams = n // TEAM
    wins = record.shape[1]
    lags = record.shape[2]
    bins = lags // 2
    chunk = wins // GROUPS
    below = team > 0
    above = team < teams - 1
    step = TEAM * (1 - 2 * odd)
    has_a = jnp.where(odd == 0, team, teams - 1 - team) > 0
    has_b = jnp.where(odd == 0, teams - 1 - team, team) > 0
    sign = (1 - 2 * odd).astype(jnp.float32)

    def block_of(slot):
        return base + jnp.where(odd == 0, slot - 2, 5 - slot)

    fetches = [
        pltpu.make_async_copy(src, dst, fetch.at[k])
        for k, (src, dst) in enumerate(
            ((table_t_in, table_t), (mask_in, mask), (table_lag_in, table_lag), (counts_in, counts)))
    ]
    for copy in fetches:
        copy.start()
    early_low = (q % 3) == 0
    first = jnp.where(early_low, 0, 2)
    barrier = pltpu.get_barrier_semaphore()
    for shift in (-1, 0, 1):
        for i in range(TEAM):
            other = base + shift * TEAM + i
            there = (other >= 0) & (other < n) & (other != me)

            @pl.when(there)
            def _():
                pl.semaphore_signal(barrier, inc=1, device_id={axis: other})

    def windows(g):
        return pl.ds(g * chunk, chunk)

    def lanes(i):
        return pl.ds(pl.multiple_of(i * LANES, LANES), LANES)

    def trace_copy(peer, g):
        return pltpu.make_async_remote_copy(
            src_ref=traces.at[0, windows(g), :, lanes(peer)],
            dst_ref=record.at[q, windows(g)],
            send_sem=t_send.at[peer, g],
            recv_sem=t_recv.at[q, g],
            device_id={axis: base + peer},
        )

    def own_copy(g):
        return pltpu.make_async_copy(traces.at[0, windows(g), :, lanes(q)], record.at[q, windows(g)], t_recv.at[q, g])

    peers = ((q + 2) % TEAM, 3 - q, q + 1 - 2 * odd)
    for g in range(GROUPS):
        own_copy(g).start()

    def to_a(u, g):
        return pltpu.make_async_remote_copy(
            src_ref=white.at[u + 2, windows(g)],
            dst_ref=white.at[u + 6, windows(g)],
            send_sem=z_send.at[u, g],
            recv_sem=z_recv.at[u + 2, g],
            device_id={axis: me - step},
        )

    def to_b(u, g):
        return pltpu.make_async_remote_copy(
            src_ref=white.at[u + 2, windows(g)],
            dst_ref=white.at[u - 2, windows(g)],
            send_sem=z_send.at[u + 1, g],
            recv_sem=z_recv.at[u - 2, g],
            device_id={axis: me + step},
        )

    own_slot = jnp.where(odd == 0, q, 3 - q)

    def whiten_block(u, g):
        i = jnp.where(odd == 0, u, 3 - u)
        pltpu.make_async_copy(record.at[i, windows(g)], record.at[i, windows(g)], t_recv.at[i, g]).wait()
        for h in range(0, chunk, 2):
            w = g * chunk + h
            rec = jnp.concatenate([record[i, w], record[i, w + 1]], axis=1)
            raw = jnp.dot(table_t[...], rec, preferred_element_type=jnp.float32)
            power = jnp.sum(raw * raw, axis=0, keepdims=True) / bins
            inv = 1.0 / jnp.sqrt(power + 1e-06)
            for e in range(2):
                part = slice(e * LANES, (e + 1) * LANES)
                keep = mask[base + i, w + e].astype(jnp.float32)
                white[u + 2, w + e] = (raw[:, part] * (inv[:, part] * keep)).astype(jnp.bfloat16)

    def pass_on(u, g):
        @pl.when((u <= 2) & has_a)
        def _():
            to_a(u, g).start()

        @pl.when((u >= 2) & has_b)
        def _():
            to_b(u, g).start()

    def block_chunks(u, start):
        def one(g, carry):
            whiten_block(u, g)
            pass_on(u, g)
            return carry

        lax.fori_loop(start, GROUPS, one, 0)

    def stack_run(run, g):
        s, t0, count = run
        place = FIRST[run]

        def one(v, carry):
            t = t0 + v

            def tile(k, inner):
                re_at = pl.ds(pl.multiple_of(k * TILE, TILE), TILE)
                im_at = pl.ds(pl.multiple_of(bins + k * TILE, TILE), TILE)
                fresh = g == 0
                real = jnp.where(fresh, 0.0, acc[place + v, re_at, :])
                imag = jnp.where(fresh, 0.0, acc[place + v, im_at, :])
                for h in range(chunk):
                    w = g * chunk + h
                    a_re = white[s, w, re_at, :].astype(jnp.float32)
                    a_im = white[s, w, im_at, :].astype(jnp.float32)
                    b_re = white[t, w, re_at, :].astype(jnp.float32)
                    b_im = white[t, w, im_at, :].astype(jnp.float32)
                    real = real + (a_re * b_re + a_im * b_im)
                    imag = imag + (a_im * b_re - a_re * b_im)
                acc[place + v, re_at, :] = real
                acc[place + v, im_at, :] = imag
                return inner

            lax.fori_loop(0, bins // TILE, tile, 0)
            return carry

        lax.fori_loop(0, count, one, 0)

    def result_copies(s, t, index):
        early = block_of(jnp.where(odd == 0, s, t))
        late = block_of(jnp.where(odd == 0, t, s))
        out = []
        for side, owner in ((0, early), (1, late)):
            src = res.at[index, pl.ds(side * bins, bins)]
            dst = back.at[side, t - s - 1, :, lanes(q)]
            local = pltpu.make_async_copy(src, dst, r_recv.at[side, t - s - 1])
            remote = pltpu.make_async_remote_copy(
                src_ref=src, dst_ref=dst, send_sem=r_send.at[index, side],
                recv_sem=r_recv.at[side, t - s - 1], device_id={axis: owner},
            )
            out.append((owner, local, remote))
        return out

    def finish_run(run):
        s, t0, count = run
        place = FIRST[run]

        def one(v, carry):
            total = acc[place + v] * (1.0 / math.sqrt(wins))
            stacked = jnp.concatenate([total[:bins], total[bins:] * sign], axis=0).astype(jnp.bfloat16)
            corr = jnp.dot(table_lag[...], stacked, preferred_element_type=jnp.float32) * (1.0 / math.sqrt(bins))
            res[place + v] = corr.astype(jnp.bfloat16)
            for owner, local, remote in result_copies(s, t0 + v, place + v):
                @pl.when(owner == me)
                def _():
                    local.start()

                @pl.when(owner != me)
                def _():
                    remote.start()
            return carry

        lax.fori_loop(0, count, one, 0)

    def finish_sends(run):
        s, t0, count = run
        place = FIRST[run]

        def one(v, carry):
            for owner, local, remote in result_copies(s, t0 + v, place + v):
                @pl.when(owner != me)
                def _():
                    remote.wait_send()
            return carry

        lax.fori_loop(0, count, one, 0)

    def arrived(z, slot, g):
        view = white.at[slot, windows(g)]
        pltpu.make_async_copy(view, view, z_recv.at[z, g]).wait()

    def far(g, carry):
        for v in range(2):
            whiten_block(2 - first + v, g)
            pass_on(2 - first + v, g)
        for run in OWN_PAIRS:
            stack_run(run, g)
        return carry

    for copy in fetches[:2]:
        copy.wait()
    whiten_block(own_slot, 0)
    pl.semaphore_wait(barrier, TEAM - 1 + TEAM * below.astype(jnp.int32) + TEAM * above.astype(jnp.int32))
    pass_on(own_slot, 0)
    for g in range(GROUPS):
        for peer in peers:
            trace_copy(peer, g).start()
    block_chunks(own_slot, 1)
    block_chunks(2 * first + 1 - own_slot, 0)
    lax.fori_loop(0, GROUPS, far, 0)
    fetches[2].wait()
    for run in OWN_PAIRS:
        finish_run(run)

    def group(ready, zs, runs):
        @pl.when(ready)
        def _():
            def one(g, carry):
                for z in zs:
                    arrived(z, z if z < 2 else z + 4, g)
                for run in runs:
                    stack_run(run, g)

                    @pl.when(g == GROUPS - 1)
                    def _():
                        finish_run(run)
                return carry

            lax.fori_loop(0, GROUPS, one, 0)

    def half(p, carry):
        low = (p == 0) == early_low
        group(low & has_b, (2, 3), B_PAIRS)
        group(jnp.logical_not(low) & has_a, (0, 1), A_PAIRS)
        group(jnp.logical_not(low) & has_b, (4,), C_PAIRS)
        return carry

    lax.fori_loop(0, 2, half, 0)
    group(has_a & has_b, (), AB_PAIRS)

    def sent(g, carry):
        for peer in peers:
            trace_copy(peer, g).wait_send()

        @pl.when(has_a)
        def _():
            for u in range(3):
                to_a(u, g).wait_send()

        @pl.when(has_b)
        def _():
            for u in range(2, 4):
                to_b(u, g).wait_send()

        return carry

    lax.fori_loop(0, GROUPS, sent, 0)
    fetches[3].wait()
    for j in range(MAXP):
        for side, there in ((0, me + j + 1 < n), (1, me - j - 1 >= 0)):
            @pl.when(there)
            def _():
                view = back.at[side, j]
                pltpu.make_async_copy(view, view, r_recv.at[side, j]).wait()
        reach = counts[me] >= j + 1
        ready[0, j] = jnp.where(reach, back[0, j], jnp.bfloat16(0))
        pltpu.make_async_copy(ready.at[0, j], fwd_out.at[0, j], o_sem.at[0, j]).start()
        source = jnp.maximum(me - j - 1, 0)
        reached = (counts[source] >= j + 1) & (me >= j + 1)
        ready[1, j] = jnp.where(reached, back[1, j], jnp.bfloat16(0))
        pltpu.make_async_copy(ready.at[1, j], bwd_out.at[0, j], o_sem.at[1, j]).start()
    for run in OWN_PAIRS:
        finish_sends(run)

    @pl.when(has_a)
    def _():
        for run in A_PAIRS:
            finish_sends(run)

    @pl.when(has_b)
    def _():
        for run in B_PAIRS + C_PAIRS:
            finish_sends(run)

    @pl.when(has_a & has_b)
    def _():
        for run in AB_PAIRS:
            finish_sends(run)
    for j in range(MAXP):
        pltpu.make_async_copy(ready.at[0, j], fwd_out.at[0, j], o_sem.at[0, j]).wait()
        pltpu.make_async_copy(ready.at[1, j], bwd_out.at[0, j], o_sem.at[1, j]).wait()


def widen(fwd, bwd, fwd_out, bwd_out):
    fwd_out[...] = fwd[...].astype(jnp.float32)
    bwd_out[...] = bwd[...].astype(jnp.float32)


def local(traces, mask, counts):
    axis = "chan"
    n = lax.axis_size(axis)
    _, wins, lags, width = traces.shape
    bins = lags // 2
    table = lag_table(lags, bins)
    table_lag = np.concatenate([table[:bins], table[bins:][::-1]], axis=0)
    half = jax.ShapeDtypeStruct((1, MAXP, bins, width), jnp.bfloat16)
    forward, backward = pl.pallas_call(
        functools.partial(kernel, axis, n),
        out_shape=(half, half),
        in_specs=[pl.BlockSpec(memory_space=pltpu.HBM)] * 5,
        out_specs=[pl.BlockSpec(memory_space=pltpu.HBM)] * 2,
        scratch_shapes=[
            pltpu.SMEM(mask.shape, jnp.int32),
            pltpu.SMEM(counts.shape, jnp.int32),
            pltpu.VMEM((lags, lags), jnp.bfloat16),
            pltpu.VMEM((lags, lags), jnp.bfloat16),
            pltpu.SemaphoreType.DMA((4,)),
            pltpu.VMEM((TEAM, wins, lags, LANES), jnp.bfloat16),
            pltpu.VMEM((SLOTS, wins, lags, LANES), jnp.bfloat16),
            pltpu.VMEM((PAIRS, lags, LANES), jnp.float32),
            pltpu.VMEM((PAIRS, lags, LANES), jnp.bfloat16),
            pltpu.VMEM((2, MAXP, bins, width), jnp.bfloat16),
            pltpu.VMEM((2, MAXP, bins, width), jnp.bfloat16),
            pltpu.SemaphoreType.DMA((2, MAXP)),
            pltpu.SemaphoreType.DMA((TEAM, GROUPS)),
            pltpu.SemaphoreType.DMA((TEAM, GROUPS)),
            pltpu.SemaphoreType.DMA((5, GROUPS)),
            pltpu.SemaphoreType.DMA((5, GROUPS)),
            pltpu.SemaphoreType.DMA((PAIRS, 2)),
            pltpu.SemaphoreType.DMA((2, MAXP)),
        ],
        compiler_params=pltpu.CompilerParams(collective_id=0, has_side_effects=True, vmem_limit_bytes=60 << 20),
        name="xcorr",
    )(traces, mask, counts, jnp.asarray(table.T, jnp.bfloat16), jnp.asarray(table_lag, jnp.bfloat16))
    lag_block = pl.BlockSpec((1, SPAN, bins, width), lambda j: (0, j, 0, 0))
    wide = jax.ShapeDtypeStruct(half.shape, jnp.float32)
    return pl.pallas_call(
        widen,
        grid=(MAXP // SPAN,),
        out_shape=(wide, wide),
        in_specs=[lag_block, lag_block],
        out_specs=(lag_block, lag_block),
        name="widen",
    )(forward, backward)


def solution(mesh):
    return jax.shard_map(
        local,
        mesh=mesh,
        in_specs=(P(("grp", "chan"), None, None, None), P("grp", None), P("grp")),
        out_specs=(P(("grp", "chan"), None, None, None), P(("grp", "chan"), None, None, None)),
        check_vma=False,
    )
```
